256 devices in a mesh: corner: 16 (over y, x_lo, core), tm: 16 (over z, x_hi).
Axes of the slice: x: 4 (x_hi: 2, x_lo: 2; x = x_hi * 2 + x_lo), y: 4, z: 8, core: 2. Of those that a mesh axis runs over, the one named last changes fastest.
Arguments:
- signal: bfloat16 [16, 64, 65536], P('corner', None, 'tm'), may hold values from -6 to 6
- dilated_conv_weight: bfloat16 [2, 256, 128], replicated, may hold values from -0.5 to 0.5
- dilated_conv_bias: float32 [2, 256], replicated, may hold values from -3 to 3
- projection_weight: bfloat16 [2, 128, 128], replicated, may hold values from -0.5 to 0.5
- projection_bias: float32 [2, 128], replicated, may hold values from -3 to 3
- cot_top: bfloat16 [16, 64, 65536], P('corner', None, 'tm'), may hold values from -6 to 6
- cot_skip: bfloat16 [16, 64, 65536], P('corner', None, 'tm'), may hold values from -6 to 6
Outputs:
- x_top: bfloat16 [16, 64, 65536], P('corner', None, 'tm')
- skip_sum: bfloat16 [16, 64, 65536], P('corner', None, 'tm')
- grad_input: bfloat16 [16, 64, 65536], P('corner', None, 'tm')
- grad_conv: float32 [2, 256, 128], replicated
- grad_conv_bias: float32 [2, 256], replicated
- grad_out: float32 [2, 128, 128], replicated
- grad_out_bias: float32 [2, 128], replicated
The draws below stay inside these ranges and needn't reach their ends.
All inputs are finite; a program needn't handle non-finite values.
Results may differ from the reference program's by a relative error of at most 0.0065.
Values may be sent and summed in bfloat16 or wider, within the bound.
No kernel may reach another device: no remote copies, remote signals or barrier semaphores. Data moves between devices by JAX's collectives and lax.ppermute only.
A program may use at most 64 MiB of HBM per device.

```python
import math
import jax
import jax.numpy as jnp
from jax import lax

R = 64
G = 128
SKIP = 64
LAYERS = 2
CORNERS = 16
TIME = 65536
LOWER_DILATION = 4096
UPPER_DILATION = 8192


def levels(key, dims, cuts, smallest, largest):
    level, own = 1.0, jax.random.fold_in(key, 6)
    for position, parts in cuts:
        steps = jnp.exp(jax.random.uniform(jax.random.fold_in(own, position), (parts,), jnp.float32, smallest / len(cuts), largest / len(cuts)))
        level = level * jnp.repeat(steps, dims[position] // parts).reshape([-1 if axis == position else 1 for axis in range(len(dims))])
    return level


def scatter_about(rng, extent, spread, limit, cuts=(), kind=jnp.bfloat16):
    factor_of = levels(rng, extent, cuts, -0.22, 0.18) if cuts else 1.0
    array = jax.random.normal(rng, extent, jnp.float32) * spread * factor_of
    return jnp.minimum(jnp.maximum(array, -limit), limit).astype(kind)


def setup_inputs(seed: int = 0) -> dict:
    key_list = jax.random.split(jax.random.key(seed), 8)
    signal = scatter_about(key_list[0], (CORNERS, R, TIME), 1.0, 6.0, ((0, 16), (2, 16)))
    dilated_conv_weight = scatter_about(key_list[1], (LAYERS, 2 * G, 2 * R), (2 * R) ** -0.5, 0.5)
    dilated_conv_bias = scatter_about(key_list[2], (LAYERS, 2 * G), 0.5, 3.0, (), jnp.float32)
    projection_weight = scatter_about(key_list[3], (LAYERS, R + SKIP, G), G ** -0.5, 0.5)
    projection_bias = scatter_about(key_list[4], (LAYERS, R + SKIP), 0.5, 3.0, (), jnp.float32)
    cot_top = scatter_about(key_list[5], (CORNERS, R, TIME), 1.0, 6.0, ((0, 16), (2, 16)))
    cot_skip = scatter_about(key_list[6], (CORNERS, SKIP, TIME), 1.0, 6.0, ((0, 16), (2, 16)))
    return dict(signal=signal, dilated_conv_weight=dilated_conv_weight, dilated_conv_bias=dilated_conv_bias, projection_weight=projection_weight, projection_bias=projection_bias, cot_top=cot_top, cot_skip=cot_skip)


def shift_delayed(field, shift):
    zeros = jnp.zeros((field.shape[0], shift), field.dtype)
    return jnp.concatenate([zeros, field[:, :field.shape[1] - shift]], axis=1)

def shift_forward(field, shift):
    zeros = jnp.zeros((field.shape[0], shift), field.dtype)
    return jnp.concatenate([field[:, shift:], zeros], axis=1)

def gated_layer_forward(a_in, tap_in, weight, bias, proj, proj_bias):
    stacked = jnp.concatenate([tap_in, a_in], axis=0)
    pre_act = jnp.dot(weight, stacked, preferred_element_type=jnp.float32) + bias[:, None]
    gate_out = (jnp.tanh(pre_act[:G]) * jax.nn.sigmoid(pre_act[G:])).astype(jnp.bfloat16)
    mixed = jnp.dot(proj, gate_out, preferred_element_type=jnp.float32) + proj_bias[:, None]
    next_act = (a_in.astype(jnp.float32) + mixed[:R]).astype(jnp.bfloat16)
    return (stacked, pre_act, gate_out, next_act, mixed[R:])

def layer_backward(go_res, go_skip, stacked, pre_act, gate_out, weight, proj):
    upper = jnp.concatenate([go_res, go_skip], axis=0)
    grad_proj = jnp.dot(upper, gate_out.T, preferred_element_type=jnp.float32)
    grad_pbias = lax.optimization_barrier(jnp.sum(upper.astype(jnp.float32), axis=1))
    grad_gate = jnp.dot(proj.T, upper, preferred_element_type=jnp.float32)
    filt_act = jnp.tanh(pre_act[:G])
    gate_act = jax.nn.sigmoid(pre_act[G:])
    grad_pre = jnp.concatenate([grad_gate * gate_act * (1.0 - filt_act * filt_act), grad_gate * filt_act * gate_act * (1.0 - gate_act)], axis=0).astype(jnp.bfloat16)
    grad_weight = jnp.dot(grad_pre, stacked.T, preferred_element_type=jnp.float32)
    grad_bias = lax.optimization_barrier(jnp.sum(grad_pre.astype(jnp.float32), axis=1))
    grad_in = jnp.dot(weight.T, grad_pre, preferred_element_type=jnp.float32)
    return (grad_in[:R].astype(jnp.bfloat16), grad_in[R:], grad_weight, grad_bias, grad_proj, grad_pbias)

def reference(signal, dilated_conv_weight, dilated_conv_bias, projection_weight, projection_bias, cot_top, cot_skip):

    def one_corner(items):
        lower_layer_input, upper_output_gradient, skip_cot = items
        lower_saved_state, lower_preactivation, lower_gated_output, middle_layer_input, lower_skip_output = gated_layer_forward(lower_layer_input, shift_delayed(lower_layer_input, LOWER_DILATION), dilated_conv_weight[0], dilated_conv_bias[0], projection_weight[0], projection_bias[0])
        upper_saved_state, upper_preactivation, upper_gated_output, upper_layer_output, upper_skip_output = gated_layer_forward(middle_layer_input, shift_delayed(middle_layer_input, UPPER_DILATION), dilated_conv_weight[1], dilated_conv_bias[1], projection_weight[1], projection_bias[1])
        skip_out = (lower_skip_output + upper_skip_output).astype(jnp.bfloat16)
        delayed_gradient_upper, current_gradient_upper, gw_top, gb_top, gv_top, gcb_top = layer_backward(upper_output_gradient, skip_cot, upper_saved_state, upper_preactivation, upper_gated_output, dilated_conv_weight[1], projection_weight[1])
        middle_input_gradient = (upper_output_gradient.astype(jnp.float32) + current_gradient_upper + shift_forward(delayed_gradient_upper, UPPER_DILATION).astype(jnp.float32)).astype(jnp.bfloat16)
        delayed_gradient_lower, current_gradient_lower, gw_low, gb_low, gv_low, gcb_low = layer_backward(middle_input_gradient, skip_cot, lower_saved_state, lower_preactivation, lower_gated_output, dilated_conv_weight[0], projection_weight[0])
        lower_input_gradient = (middle_input_gradient.astype(jnp.float32) + current_gradient_lower + shift_forward(delayed_gradient_lower, LOWER_DILATION).astype(jnp.float32)).astype(jnp.bfloat16)
        return (upper_layer_output, skip_out, lower_input_gradient, jnp.stack([gw_low, gw_top]), jnp.stack([gb_low, gb_top]), jnp.stack([gv_low, gv_top]), jnp.stack([gcb_low, gcb_top]))
    outs = lax.map(one_corner, (signal, cot_top, cot_skip))
    scale = 1.0 / math.sqrt(CORNERS * TIME)
    return (outs[0], outs[1], outs[2], lax.optimization_barrier(jnp.sum(outs[3], axis=0)) * scale, lax.optimization_barrier(jnp.sum(outs[4], axis=0)) * scale, lax.optimization_barrier(jnp.sum(outs[5], axis=0)) * scale, lax.optimization_barrier(jnp.sum(outs[6], axis=0)) * scale)
```

```python
import math

import jax
import jax.numpy as jnp
from jax import lax
from jax.sharding import Mesh, PartitionSpec as P

CORNER = ("y", "xl", "core")
TM = ("z", "xh")
CHIPS = ("y", "xl", "z", "xh")


def from_behind(block, axis, distance):
    devices = range(lax.axis_size(axis))
    route = [(i - distance, i) for i in devices if i - distance in devices]
    return lax.ppermute(block, axis, route)


def swap_cores(block):
    return lax.ppermute(block, "core", [(0, 1), (1, 0)])


def pack_layer(grads):
    weight, bias, proj, proj_bias = grads
    rows = jnp.concatenate(
        [weight, proj, bias.reshape(-1, 128), proj_bias.reshape(-1, 128)], axis=0
    )
    chips = lax.axis_size(CHIPS)
    each = -(-rows.shape[0] // (4 * chips)) * 4
    return jnp.pad(rows, ((0, each * chips - rows.shape[0]), (0, 0)))


def unpack_layer(rows):
    return rows[:256], rows[384:386].reshape(256), rows[256:384], rows[386]


def reduce_over_chips(rows):
    chips = lax.axis_size(CHIPS)
    parts = rows.reshape(chips, -1, 128)
    share = jnp.sum(lax.all_to_all(parts, CHIPS, 0, 0, tiled=True), axis=0, keepdims=True)
    whole = lax.all_to_all(jnp.broadcast_to(share, parts.shape), CHIPS, 0, 0, tiled=True)
    return whole.reshape(rows.shape)


def gated_layer_forward(a_in, tap_in, weight, bias, proj, proj_bias, gsize, rsize):
    stacked = jnp.concatenate([tap_in, a_in], axis=1)
    pre_act = (
        jnp.einsum("oc,bct->bot", weight, stacked, preferred_element_type=jnp.float32)
        + bias[None, :, None]
    )
    gate_out = (jnp.tanh(pre_act[:, :gsize]) * jax.nn.sigmoid(pre_act[:, gsize:])).astype(
        jnp.bfloat16
    )
    mixed = (
        jnp.einsum("og,bgt->bot", proj, gate_out, preferred_element_type=jnp.float32)
        + proj_bias[None, :, None]
    )
    next_act = (a_in.astype(jnp.float32) + mixed[:, :rsize]).astype(jnp.bfloat16)
    return (stacked, pre_act, gate_out, next_act, mixed[:, rsize:])


def layer_backward(go_res, go_skip, stacked, pre_act, gate_out, weight, proj, gsize, rsize):
    upper = jnp.concatenate([go_res, go_skip], axis=1)
    grad_proj = jnp.einsum("bot,bgt->og", upper, gate_out, preferred_element_type=jnp.float32)
    grad_pbias = jnp.sum(upper, axis=(0, 2), dtype=jnp.float32)
    grad_gate = jnp.einsum("og,bot->bgt", proj, upper, preferred_element_type=jnp.float32)
    filt_act = jnp.tanh(pre_act[:, :gsize])
    gate_act = jax.nn.sigmoid(pre_act[:, gsize:])
    grad_pre = jnp.concatenate(
        [
            grad_gate * gate_act * (1.0 - filt_act * filt_act),
            grad_gate * filt_act * gate_act * (1.0 - gate_act),
        ],
        axis=1,
    ).astype(jnp.bfloat16)
    grad_weight = jnp.einsum("bot,bct->oc", grad_pre, stacked, preferred_element_type=jnp.float32)
    grad_bias = jnp.sum(grad_pre, axis=(0, 2), dtype=jnp.float32)
    grad_in = jnp.einsum("oc,bot->bct", weight, grad_pre, preferred_element_type=jnp.float32)
    return (
        grad_in[:, :rsize].astype(jnp.bfloat16),
        grad_in[:, rsize:],
        (grad_weight, grad_bias, grad_proj, grad_pbias),
    )


def on_device(
    signal,
    dilated_conv_weight,
    dilated_conv_bias,
    projection_weight,
    projection_bias,
    cot_top,
    cot_skip,
):
    rsize = signal.shape[1]
    gsize = projection_weight.shape[2]
    tap_near = from_behind(signal, TM, 1)
    (
        lower_saved_state,
        lower_preactivation,
        lower_gated_output,
        middle_layer_input,
        lower_skip_output,
    ) = gated_layer_forward(
        signal,
        tap_near,
        dilated_conv_weight[0],
        dilated_conv_bias[0],
        projection_weight[0],
        projection_bias[0],
        gsize,
        rsize,
    )
    tap_far = from_behind(middle_layer_input, TM, 2)
    (
        upper_saved_state,
        upper_preactivation,
        upper_gated_output,
        upper_layer_output,
        upper_skip_output,
    ) = gated_layer_forward(
        middle_layer_input,
        tap_far,
        dilated_conv_weight[1],
        dilated_conv_bias[1],
        projection_weight[1],
        projection_bias[1],
        gsize,
        rsize,
    )
    skip_out = (lower_skip_output + upper_skip_output).astype(jnp.bfloat16)
    delayed_gradient_upper, current_gradient_upper, grads_top = layer_backward(
        cot_top,
        cot_skip,
        upper_saved_state,
        upper_preactivation,
        upper_gated_output,
        dilated_conv_weight[1],
        projection_weight[1],
        gsize,
        rsize,
    )
    later_top = from_behind(delayed_gradient_upper, TM, -2)
    middle_input_gradient = (
        cot_top.astype(jnp.float32) + current_gradient_upper + later_top.astype(jnp.float32)
    ).astype(jnp.bfloat16)
    delayed_gradient_lower, current_gradient_lower, grads_low = layer_backward(
        middle_input_gradient,
        cot_skip,
        lower_saved_state,
        lower_preactivation,
        lower_gated_output,
        dilated_conv_weight[0],
        projection_weight[0],
        gsize,
        rsize,
    )
    later_low = from_behind(delayed_gradient_lower, TM, -1)
    lower_input_gradient = (
        middle_input_gradient.astype(jnp.float32)
        + current_gradient_lower
        + later_low.astype(jnp.float32)
    ).astype(jnp.bfloat16)
    low, top = pack_layer(grads_low), pack_layer(grads_top)
    mine = lax.axis_index("core") == 0
    held = jnp.where(mine, low, top) + swap_cores(jnp.where(mine, top, low))
    held = reduce_over_chips(held)
    other = swap_cores(held)
    count = signal.shape[0] * lax.axis_size(CORNER) * signal.shape[2] * lax.axis_size(TM)
    scale = 1.0 / math.sqrt(count)
    low, top = jnp.where(mine, held, other), jnp.where(mine, other, held)
    grads = [jnp.stack(pair) * scale for pair in zip(unpack_layer(low), unpack_layer(top))]
    return (upper_layer_output, skip_out, lower_input_gradient, *grads)


def solution(mesh):
    fine = Mesh(mesh.devices.reshape(4, 2, 2, 8, 2), ("y", "xl", "core", "z", "xh"))
    field = P(CORNER, None, TM)
    return jax.shard_map(
        on_device,
        mesh=fine,
        in_specs=(field, P(), P(), P(), P(), field, field),
        out_specs=(field, field, field, P(), P(), P(), P()),
        check_vma=False,
    )
```

```python
import math

import jax
import jax.numpy as jnp
from jax import lax
from jax.experimental import pallas as pl
from jax.experimental.pallas import tpu as pltpu
from jax.sharding import Mesh, PartitionSpec as P

CORNER = ("y", "xl", "core")
TM = ("z", "xh")
CHIPS = ("y", "xl", "z", "xh")
HALVES = 2
TILE = 512
F32, BF16 = jnp.float32, jnp.bfloat16


def from_behind(block, distance):
    devices = range(lax.axis_size(TM))
    route = [(i - distance, i) for i in devices if i - distance in devices]
    return lax.ppermute(block, TM, route)


def mm(a, b):
    return lax.dot_general(a, b, (((1,), (0,)), ((), ())), preferred_element_type=F32)


def mm_t(a, b):
    return lax.dot_general(a, b, (((1,), (1,)), ((), ())), preferred_element_type=F32)


def gates(weight, stacked, bias):
    pre = mm(weight, stacked) + bias
    half = pre.shape[0] // 2
    return jnp.tanh(pre[:half]), 0.5 * jnp.tanh(0.5 * pre[half:]) + 0.5


def gate_grad(gz, filt, gate):
    both = gz * gate
    return jnp.concatenate(
        [both * (1.0 - filt * filt), both * filt * (1.0 - gate)], axis=0
    ).astype(BF16)


def tiles(n):
    return [slice(i, i + TILE) for i in range(0, n, TILE)]


def shift(s, off):
    return slice(s.start + off, s.stop + off)


def call(body, out, flops, name, *args):
    size = sum(math.prod(a.shape) * a.dtype.itemsize for a in (*args, *out))
    spec = pl.BlockSpec(memory_space=pltpu.VMEM)
    return pl.pallas_call(
        body,
        out_shape=[jax.ShapeDtypeStruct(o.shape, o.dtype) for o in out],
        in_specs=[spec] * len(args),
        out_specs=[spec] * len(out),
        name=name,
        cost_estimate=pl.CostEstimate(
            flops=flops, bytes_accessed=size, transcendentals=0
        ),
        compiler_params=pltpu.CompilerParams(vmem_limit_bytes=12 * 2**20),
    )(*args)


def arr(*shape, dtype=BF16):
    return jax.ShapeDtypeStruct(shape, dtype)


def lower_forward(off, n, signal, tap, w, b, v, vb):
    def body(sig, tap, w, b, v, vb, mid, z_out):
        for s in tiles(n):
            a = sig[0, :, shift(s, off)]
            filt, gate = gates(w[0], jnp.concatenate([tap[:, s], a], axis=0), b[0])
            z = (filt * gate).astype(BF16)
            z_out[:, s] = z
            mid[:, s] = (a.astype(F32) + mm(v[0, :64, :], z) + vb[0, :64, :]).astype(BF16)

    return call(
        body, [arr(64, n), arr(128, n)], 90000 * n, "lower_forward", signal, tap, w, b, v, vb
    )


def upper_critical(off, n, mid, tap, top, skip, w, b, wt, vt):
    def body(mid, tap, top, skip, w, b, wt, vt, z_out, gpre_out, gdel):
        for s in tiles(n):
            filt, gate = gates(w[1], jnp.concatenate([tap[:, s], mid[:, s]], axis=0), b[1])
            z_out[:, s] = (filt * gate).astype(BF16)
            u = jnp.concatenate([top[0, :, shift(s, off)], skip[0, :, shift(s, off)]], axis=0)
            gpre = gate_grad(mm(vt[1], u), filt, gate)
            gpre_out[:, s] = gpre
            gdel[:, s] = mm(wt[1, :64, :], gpre).astype(BF16)

    return call(
        body,
        [arr(128, n), arr(256, n), arr(64, n)],
        130000 * n,
        "upper_critical",
        mid, tap, top, skip, w, b, wt, vt,
    )


def put_sums(out, gpre, u, stacked, z, before=None):
    ones = jnp.ones((16, u.shape[1]), BF16)
    bias, proj_bias = mm_t(ones, gpre), mm_t(ones, u)
    rows = [
        (0, mm_t(gpre, stacked)),
        (256, mm_t(u, z)),
        (384, jnp.concatenate([bias[:1, :128], bias[:1, 128:], proj_bias[:1]], axis=0)),
    ]
    for start, value in rows:
        at = slice(start, start + value.shape[0])
        out[at, :] = value if before is None else before[at, :] + value


def upper_rest(n, mids, taps, gpres, z0s, z1s, top, skip, v, vb):
    h = len(mids)

    def body(*refs):
        mids, taps, gpres, z0s, z1s = (refs[i * h : i * h + h] for i in range(5))
        top, skip, v, vb, x_top, skip_sum, sums, u, st, gp, z1 = refs[5 * h :]
        both = jnp.concatenate([v[0, 64:, :], v[1, 64:, :]], axis=1)
        both_bias = vb[0, 64:, :] + vb[1, 64:, :]
        for i in range(h):
            for s in tiles(n):
                at = shift(s, i * n)
                z = z1s[i][:, s]
                mid = mids[i][:, s]
                x_top[0, :, at] = (mid.astype(F32) + mm(v[1, :64, :], z) + vb[1, :64, :]).astype(BF16)
                zz = jnp.concatenate([z0s[i][:, s], z], axis=0)
                skip_sum[0, :, at] = (mm(both, zz) + both_bias).astype(BF16)
                u[:64, at] = top[0, :, at]
                u[64:, at] = skip[0, :, at]
                st[:64, at] = taps[i][:, s]
                st[64:, at] = mid
                gp[:, at] = gpres[i][:, s]
                z1[:, at] = z
        sums[384:, :] = jnp.zeros((sums.shape[0] - 384, 128), F32)
        put_sums(sums, gp[...], u[...], st[...], z1[...])

    m = h * n
    args = (*mids, *taps, *gpres, *z0s, *z1s, top, skip, v, vb)
    out = [arr(1, 64, m), arr(1, 64, m), arr(512, 128, dtype=F32)]
    size = sum(math.prod(a.shape) * a.dtype.itemsize for a in (*args, *out))
    spec = pl.BlockSpec(memory_space=pltpu.VMEM)
    return pl.pallas_call(
        body,
        out_shape=out,
        in_specs=[spec] * len(args),
        out_specs=[spec] * 3,
        scratch_shapes=[pltpu.VMEM((k, m), BF16) for k in (128, 128, 256, 128)],
        name="upper_rest",
        cost_estimate=pl.CostEstimate(flops=200000 * m, bytes_accessed=size, transcendentals=0),
        compiler_params=pltpu.CompilerParams(vmem_limit_bytes=12 * 2**20),
    )(*args)


def lower_backward(off, n, gdel, gpre1, signal, tap, z0, top, skip, w, b, wt, vt, before):
    def body(gdel, gpre1, sig, tap, z0, top, skip, w, b, wt, vt, *rest):
        before, (mid_grad, gpre_out, sums, u, st) = rest[:-5], rest[-5:]
        for s in tiles(n):
            at = shift(s, off)
            grad = (
                top[0, :, at].astype(F32) + mm(wt[1, 64:, :], gpre1[:, s]) + gdel[:, s].astype(F32)
            ).astype(BF16)
            mid_grad[:, s] = grad
            both = jnp.concatenate([grad, skip[0, :, at]], axis=0)
            u[:, s] = both
            stacked = jnp.concatenate([tap[:, s], sig[0, :, at]], axis=0)
            st[:, s] = stacked
            filt, gate = gates(w[0], stacked, b[0])
            gpre_out[:, s] = gate_grad(mm(vt[0], both), filt, gate)
        sums[384:, :] = jnp.zeros((sums.shape[0] - 384, 128), F32)
        put_sums(sums, gpre_out[...], u[...], st[...], z0[...], *before)

    args = (gdel, gpre1, signal, tap, z0, top, skip, w, b, wt, vt, *before)
    out = [arr(64, n), arr(256, n), arr(512, 128, dtype=F32)]
    size = sum(math.prod(a.shape) * a.dtype.itemsize for a in (*args, *out))
    spec = pl.BlockSpec(memory_space=pltpu.VMEM)
    return pl.pallas_call(
        body,
        out_shape=out,
        in_specs=[spec] * len(args),
        out_specs=[spec] * 3,
        scratch_shapes=[pltpu.VMEM((128, n), BF16)] * 2,
        name="lower_backward",
        cost_estimate=pl.CostEstimate(flops=260000 * n, bytes_accessed=size, transcendentals=0),
        compiler_params=pltpu.CompilerParams(vmem_limit_bytes=12 * 2**20),
    )(*args)


def lower_input(n, mid_grads, gpres, wt):
    h = len(gpres)

    def body(*refs):
        grads, gpres, wt, gdel, rest = refs[:h], refs[h : 2 * h], *refs[2 * h :]
        for i in range(h):
            for s in tiles(n):
                gin = mm(wt[0], gpres[i][:, s])
                gdel[:, shift(s, i * n)] = gin[:64].astype(BF16)
                rest[:, shift(s, i * n)] = grads[i][:, s].astype(F32) + gin[64:]

    m = h * n
    return call(
        body, [arr(64, m), arr(64, m, dtype=F32)], 65000 * m, "lower_input",
        *mid_grads, *gpres, wt,
    )


def swap_cores(block, route=((0, 1), (1, 0))):
    return lax.ppermute(block, "core", route)


def unpack_layer(rows):
    return rows[:256], rows[384:386].reshape(256), rows[256:384], rows[386]


def reduce_over_chips(rows, scale):
    chips = lax.axis_size(CHIPS)
    parts = rows.reshape(chips, -1, 128)
    share = jnp.sum(lax.all_to_all(parts, CHIPS, 0, 0, tiled=True), axis=0, keepdims=True)
    whole = lax.all_to_all(
        jnp.broadcast_to(share * scale, parts.shape), CHIPS, 0, 0, tiled=True
    )
    return whole.reshape(rows.shape)


def on_device(signal, w, b, v, vb, top, skip):
    m = signal.shape[2]
    n = m // HALVES
    offs = range(0, m, n)
    taps = [from_behind(signal[0, :, o : o + n], 1) for o in offs]
    b, vb = b[:, :, None], vb[:, :, None]
    wt, vt = jnp.swapaxes(w, 1, 2), jnp.swapaxes(v, 1, 2)
    mids, z0s, mid_taps = [], [], []
    for o, tap in zip(offs, taps):
        mid, z0 = lower_forward(o, n, signal, tap, w, b, v, vb)
        mids.append(mid)
        z0s.append(z0)
        mid_taps.append(from_behind(mid, 2))
    z1s, gpres1, gdels1 = [], [], []
    for o, mid, tap in zip(offs, mids, mid_taps):
        z1, gpre1, gdel = upper_critical(o, n, mid, tap, top, skip, w, b, wt, vt)
        z1s.append(z1)
        gpres1.append(gpre1)
        gdels1.append(from_behind(gdel, -2))
    x_top, skip_sum, high = upper_rest(n, mids, mid_taps, gpres1, z0s, z1s, top, skip, v, vb)
    high_other = swap_cores(high, [(0, 1)])
    low, mid_grads, gpres0 = [], [], []
    for i, o in enumerate(offs):
        grad, gpre0, *low = lower_backward(
            o, n, gdels1[i], gpres1[i], signal, taps[i], z0s[i], top, skip, w, b, wt, vt, low
        )
        mid_grads.append(grad)
        gpres0.append(gpre0)
    low_other = swap_cores(low[0], [(1, 0)])
    first = lax.axis_index("core") == 0
    count = signal.shape[0] * lax.axis_size(CORNER) * m * lax.axis_size(TM)
    held = reduce_over_chips(
        jnp.where(first, low[0] + low_other, high + high_other), 1.0 / math.sqrt(count)
    )
    gdel0, rest = lower_input(n, mid_grads, gpres0, wt)
    grad_input = (rest + from_behind(gdel0, -1).astype(F32)).astype(BF16)[None]
    other = swap_cores(held)
    low, high = jnp.where(first, held, other), jnp.where(first, other, held)
    grads = [jnp.stack(pair) for pair in zip(unpack_layer(low), unpack_layer(high))]
    return (x_top, skip_sum, grad_input, *grads)


def solution(mesh):
    fine = Mesh(mesh.devices.reshape(4, 2, 2, 8, 2), ("y", "xl", "core", "z", "xh"))
    field = P(CORNER, None, TM)
    return jax.shard_map(
        on_device,
        mesh=fine,
        in_specs=(field, P(), P(), P(), P(), field, field),
        out_specs=(field, field, field, P(), P(), P(), P()),
        check_vma=False,
    )
```

```python
import math

import jax
import jax.numpy as jnp
from jax import lax
from jax.experimental import pallas as pl
from jax.experimental.pallas import tpu as pltpu
from jax.sharding import Mesh, PartitionSpec as P

CORNER = ("y", "xl", "core")
TM = ("z", "xh")
PLANE = ("y", "xl", "xh")
HALVES = 2
TILE = 512
F32, BF16 = jnp.float32, jnp.bfloat16


def from_behind(block, distance):
    devices = range(lax.axis_size(TM))
    route = [(i - distance, i) for i in devices if i - distance in devices]
    return lax.ppermute(block, TM, route)


def mm(a, b):
    return lax.dot_general(a, b, (((1,), (0,)), ((), ())), preferred_element_type=F32)


def mm_t(a, b):
    return lax.dot_general(a, b, (((1,), (1,)), ((), ())), preferred_element_type=F32)


def gates(weight, stacked, bias):
    pre = mm(weight, stacked) + bias
    half = pre.shape[0] // 2
    return jnp.tanh(pre[:half]), 0.5 * jnp.tanh(0.5 * pre[half:]) + 0.5


def gate_grad(gz, filt, gate):
    both = gz * gate
    return jnp.concatenate(
        [both * (1.0 - filt * filt), both * filt * (1.0 - gate)], axis=0
    ).astype(BF16)


def tiles(n):
    return [slice(i, i + TILE) for i in range(0, n, TILE)]


def shift(s, off):
    return slice(s.start + off, s.stop + off)


def call(body, out, flops, name, *args, scratch=()):
    size = sum(math.prod(a.shape) * a.dtype.itemsize for a in (*args, *out))
    spec = pl.BlockSpec(memory_space=pltpu.VMEM)
    return pl.pallas_call(
        body,
        out_shape=out,
        in_specs=[spec] * len(args),
        out_specs=[spec] * len(out),
        scratch_shapes=scratch,
        name=name,
        cost_estimate=pl.CostEstimate(flops=flops, bytes_accessed=size, transcendentals=0),
        compiler_params=pltpu.CompilerParams(vmem_limit_bytes=12 * 2**20),
    )(*args)


def near(*shape, dtype=BF16):
    return jax.ShapeDtypeStruct(shape, dtype)


def prepare(w, b, v, vb):
    def body(w, b, v, vb, b_out, vb_out, wt, vt):
        for rows, out in ((b, b_out), (vb, vb_out)):
            out[...] = jnp.transpose(jnp.tile(rows[...], (4, 1)))
        for layer in range(2):
            wt[layer] = jnp.transpose(w[layer])
            vt[layer] = jnp.transpose(v[layer])

    out = [near(256, 8, dtype=F32), near(128, 8, dtype=F32), near(2, 128, 256), near(2, 128, 128)]
    return call(body, out, 1000, "prepare", w, b, v, vb)


def lower_forward(off, n, signal, tap, w, b, v, vb):
    def body(sig, tap, w, b, v, vb, mid, z_out):
        for s in tiles(n):
            a = sig[0, :, shift(s, off)]
            filt, gate = gates(w[0], jnp.concatenate([tap[:, s], a], axis=0), b[:, 0:1])
            z = (filt * gate).astype(BF16)
            z_out[:, s] = z
            mid[:, s] = (a.astype(F32) + mm(v[0, :64, :], z) + vb[:64, 0:1]).astype(BF16)

    out = [near(64, n), near(128, n)]
    return call(body, out, 90000 * n, "lower_forward", signal, tap, w, b, v, vb)


def upper_critical(off, n, mid, tap, top, skip, w, b, wt, vt):
    def body(mid, tap, top, skip, w, b, wt, vt, z_out, gpre_out, gdel):
        for s in tiles(n):
            filt, gate = gates(w[1], jnp.concatenate([tap[:, s], mid[:, s]], axis=0), b[:, 1:2])
            z_out[:, s] = (filt * gate).astype(BF16)
            u = jnp.concatenate([top[0, :, shift(s, off)], skip[0, :, shift(s, off)]], axis=0)
            gpre = gate_grad(mm(vt[1], u), filt, gate)
            gpre_out[:, s] = gpre
            gdel[:, s] = mm(wt[1, :64, :], gpre).astype(BF16)

    out = [near(128, n), near(256, n), near(64, n)]
    return call(body, out, 130000 * n, "upper_critical", mid, tap, top, skip, w, b, wt, vt)


def put_sums(out, gpre, u, stacked, z, before=None):
    ones = jnp.ones((16, u.shape[1]), BF16)
    bias, proj_bias = mm_t(ones, gpre), mm_t(ones, u)
    rows = [
        (0, mm_t(gpre, stacked)),
        (256, mm_t(u, z)),
        (384, jnp.concatenate([bias[:1, :128], bias[:1, 128:], proj_bias[:1]], axis=0)),
    ]
    for start, value in rows:
        at = slice(start, start + value.shape[0])
        out[at, :] = value if before is None else before[at, :] + value


def upper_sums(n, mids, taps, gpres, z1s, top, skip):
    h = len(mids)

    def body(*refs):
        mids, taps, gpres, z1s = (refs[i * h : i * h + h] for i in range(4))
        top, skip, sums, u, st, gp, z1 = refs[4 * h :]
        u[:64, :], u[64:, :] = top[0], skip[0]
        for i in range(h):
            at = slice(i * n, i * n + n)
            st[:64, at], st[64:, at] = taps[i][...], mids[i][...]
            gp[:, at], z1[:, at] = gpres[i][...], z1s[i][...]
        sums[384:, :] = jnp.zeros((sums.shape[0] - 384, 128), F32)
        put_sums(sums, gp[...], u[...], st[...], z1[...])

    m = h * n
    return call(
        body, [near(512, 128, dtype=F32)], 100000 * m, "upper_sums",
        *mids, *taps, *gpres, *z1s, top, skip,
        scratch=[pltpu.VMEM((k, m), BF16) for k in (128, 128, 256, 128)],
    )[0]


def upper_outputs(n, mids, z0s, z1s, v, vb):
    h = len(mids)

    def body(*refs):
        mids, z0s, z1s = (refs[i * h : i * h + h] for i in range(3))
        v, vb, x_top, skip_sum = refs[3 * h :]
        both = jnp.concatenate([v[0, 64:, :], v[1, 64:, :]], axis=1)
        both_bias = vb[64:, 0:1] + vb[64:, 1:2]
        for i in range(h):
            for s in tiles(n):
                at = shift(s, i * n)
                z = z1s[i][:, s]
                own = mids[i][:, s].astype(F32) + mm(v[1, :64, :], z) + vb[:64, 1:2]
                x_top[0, :, at] = own.astype(BF16)
                zz = jnp.concatenate([z0s[i][:, s], z], axis=0)
                skip_sum[0, :, at] = (mm(both, zz) + both_bias).astype(BF16)

    m = h * n
    out = [jax.ShapeDtypeStruct((1, 64, m), BF16)] * 2
    return call(body, out, 50000 * m, "upper_outputs", *mids, *z0s, *z1s, v, vb)


def lower_backward(off, n, gdel, gpre1, signal, tap, z0, top, skip, w, b, wt, vt, before):
    def body(gdel, gpre1, sig, tap, z0, top, skip, w, b, wt, vt, *rest):
        rest, (u, st, gp) = rest[:-3], rest[-3:]
        gdel_out, part = rest[len(before) : len(before) + 2]
        if before:
            gdel_out[:, :off] = rest[0][...]
        for s in tiles(n):
            at = shift(s, off)
            own = top[0, :, at].astype(F32) + mm(wt[1, 64:, :], gpre1[:, s])
            grad = (own + gdel[:, s].astype(F32)).astype(BF16)
            both = jnp.concatenate([grad, skip[0, :, at]], axis=0)
            u[:, s] = both
            stacked = jnp.concatenate([tap[:, s], sig[0, :, at]], axis=0)
            st[:, s] = stacked
            filt, gate = gates(w[0], stacked, b[:, 0:1])
            gpre = gate_grad(mm(vt[0], both), filt, gate)
            gp[:, s] = gpre
            gin = mm(wt[0], gpre)
            gdel_out[:, shift(s, gdel_out.shape[1] - n)] = gin[:64].astype(BF16)
            part[:, s] = grad.astype(F32) + gin[64:]
        if before:
            _, sums, high, _, _, give, keep = rest
            put_sums(keep, gp[...], u[...], st[...], z0[...], sums)
            keep[387:, :] = jnp.zeros((keep.shape[0] - 387, 128), F32)
            low, high = keep[...], high[...]
            own = jnp.broadcast_to(lax.axis_index("core") == 0, low.shape)
            give[...] = jnp.where(own, high, low)
            keep[...] = jnp.where(own, low, high)
        else:
            put_sums(rest[-1], gp[...], u[...], st[...], z0[...])

    out = [near(64, off + n), near(64, n, dtype=F32)]
    out += [near(512, 128, dtype=F32)] * (2 if before else 1)
    return call(
        body, out, 320000 * n, "lower_backward",
        gdel, gpre1, signal, tap, z0, top, skip, w, b, wt, vt, *before,
        scratch=[pltpu.VMEM((k, n), BF16) for k in (128, 128, 256)],
    )


def place(held, other):
    def body(held, other, conv, conv_bias, proj, proj_bias):
        a, b = held[...], other[...]
        own = jnp.broadcast_to(lax.axis_index("core") == 0, a.shape)
        for layer, rows in enumerate((jnp.where(own, a, b), jnp.where(own, b, a))):
            conv[layer] = rows[:256]
            proj[layer] = rows[256:384]
            conv_bias[layer : layer + 1, :128] = rows[384:385]
            conv_bias[layer : layer + 1, 128:] = rows[385:386]
            proj_bias[layer : layer + 1, :] = rows[386:387]

    out = [jax.ShapeDtypeStruct(d, F32) for d in ((2, 256, 128), (2, 256), (2, 128, 128), (2, 128))]
    return call(body, out, 1000, "place", held, other)


def swap_cores(block):
    return lax.ppermute(block, "core", [(0, 1), (1, 0)])


def add(x, y):
    def body(x, y, out):
        out[...] = x[...] + y[...]

    return call(body, [near(*x.shape, dtype=F32)], 1000, "add", x, y)[0]


def finish(parts, later):
    n = parts[0].shape[1]

    def body(*refs):
        far, out = refs[-2:]
        for i, own in enumerate(refs[:-2]):
            at = slice(i * n, i * n + n)
            out[0, :, at] = (own[...] + far[:, at].astype(F32)).astype(BF16)

    return call(body, [near(1, *later.shape)], 1000, "finish", *parts, later)[0]


def share_out(parts, copies, scale=1.0):
    def body(parts, out):
        total = parts[0]
        for i in range(1, parts.shape[0]):
            total += parts[i]
        total *= scale
        for i in range(copies):
            out[i] = total

    out = [near(copies, *parts.shape[1:], dtype=F32)]
    return call(body, out, 1000, "share_out", parts)[0]


def on_device(signal, w, b, v, vb, top, skip):
    m = signal.shape[2]
    n = m // HALVES
    offs = range(0, m, n)
    taps = [from_behind(signal[0, :, o : o + n], 1) for o in offs]
    b, vb, wt, vt = prepare(w, b, v, vb)
    mids, z0s, mid_taps = [], [], []
    for o, tap in zip(offs, taps):
        mid, z0 = lower_forward(o, n, signal, tap, w, b, v, vb)
        mids.append(mid)
        z0s.append(z0)
        mid_taps.append(from_behind(mid, 2))
    z1s, gpres1, gdels1 = [], [], []
    for o, mid, tap in zip(offs, mids, mid_taps):
        z1, gpre1, gdel = upper_critical(o, n, mid, tap, top, skip, w, b, wt, vt)
        z1s.append(z1)
        gpres1.append(gpre1)
        gdels1.append(from_behind(gdel, -2))
    args = [(o, n, d, g, signal, t, z, top, skip, w, b, wt, vt)
            for o, d, g, t, z in zip(offs, gdels1, gpres1, taps, z0s)]
    gdel_a, part_a, sums = lower_backward(*args[0], [])
    z1s, sums = lax.optimization_barrier((z1s, sums))
    high = upper_sums(n, mids, mid_taps, gpres1, z1s, top, skip)
    gdel0, part_b, give, keep = lower_backward(*args[1], [gdel_a, sums, high])
    count = signal.shape[0] * lax.axis_size(CORNER) * m * lax.axis_size(TM)
    plane, depth = lax.axis_size(PLANE), lax.axis_size("z")
    scale = 1.0 / math.sqrt(count)
    rows = add(keep, swap_cores(give)).reshape(plane, -1, 128)
    rows, gdel0 = lax.optimization_barrier((rows, gdel0))
    later = from_behind(gdel0, -1)
    parts = lax.all_to_all(rows, PLANE, 0, 0, tiled=True)
    x_top, skip_sum = upper_outputs(n, mids, z0s, z1s, v, vb)
    parts, x_top, skip_sum = lax.optimization_barrier((parts, x_top, skip_sum))
    parts = share_out(parts, depth)
    parts = lax.all_to_all(parts, "z", 0, 0, tiled=True)
    parts = share_out(parts, plane, scale)
    held = lax.all_to_all(parts, PLANE, 0, 0, tiled=True).reshape(give.shape)
    grad_input = finish([part_a, part_b], later)
    return (x_top, skip_sum, grad_input, *place(held, swap_cores(held)))


def solution(mesh):
    fine = Mesh(mesh.devices.reshape(4, 2, 2, 8, 2), ("y", "xl", "core", "z", "xh"))
    field = P(CORNER, None, TM)
    return jax.shard_map(
        on_device,
        mesh=fine,
        in_specs=(field, P(), P(), P(), P(), field, field),
        out_specs=(field, field, field, P(), P(), P(), P()),
        check_vma=False,
    )
```

```python
import math

import jax
import jax.numpy as jnp
from jax import lax
from jax.experimental import pallas as pl
from jax.experimental.pallas import tpu as pltpu
from jax.sharding import Mesh, PartitionSpec as P

CORNER = ("y", "xl", "core")
TM = ("z", "xh")
PLANE = ("y", "xl", "xh")
HALVES = 2
TILE = 2048
F32, BF16 = jnp.float32, jnp.bfloat16


def from_behind(block, distance):
    devices = range(lax.axis_size(TM))
    route = [(i - distance, i) for i in devices if i - distance in devices]
    return lax.ppermute(block, TM, route)


def mm(a, b):
    return lax.dot_general(a, b, (((1,), (0,)), ((), ())), preferred_element_type=F32)


def mm_t(a, b):
    return lax.dot_general(a, b, (((1,), (1,)), ((), ())), preferred_element_type=F32)


def gates(weight, stacked, bias):
    pre = mm(weight, stacked) + bias
    half = pre.shape[0] // 2
    return jnp.tanh(pre[:half]), 0.5 * jnp.tanh(0.5 * pre[half:]) + 0.5


def gate_grad(gz, filt, gate):
    both = gz * gate
    return jnp.concatenate(
        [both * (1.0 - filt * filt), both * filt * (1.0 - gate)], axis=0
    ).astype(BF16)


def tiles(n):
    return [slice(i, i + TILE) for i in range(0, n, TILE)]


def shift(s, off):
    return slice(s.start + off, s.stop + off)


def call(body, out, flops, name, *args):
    size = sum(math.prod(a.shape) * a.dtype.itemsize for a in (*args, *out))
    spec = pl.BlockSpec(memory_space=pltpu.VMEM)
    return pl.pallas_call(
        body,
        out_shape=out,
        in_specs=[spec] * len(args),
        out_specs=[spec] * len(out),
        name=name,
        cost_estimate=pl.CostEstimate(flops=flops, bytes_accessed=size, transcendentals=0),
        compiler_params=pltpu.CompilerParams(vmem_limit_bytes=12 * 2**20),
    )(*args)


def near(*shape, dtype=BF16):
    return jax.ShapeDtypeStruct(shape, dtype)


def prepare(w, b, v, vb):
    def body(w, b, v, vb, b_out, vb_out, wt, vt):
        for rows, out in ((b, b_out), (vb, vb_out)):
            out[...] = jnp.transpose(jnp.tile(rows[...], (4, 1)))
        for layer in range(2):
            wt[layer] = jnp.transpose(w[layer])
            vt[layer] = jnp.transpose(v[layer])

    out = [near(256, 8, dtype=F32), near(128, 8, dtype=F32), near(2, 128, 256), near(2, 128, 128)]
    return call(body, out, 1000, "prepare", w, b, v, vb)


def lower_forward(off, n, signal, tap, w, b, v, vb):
    def body(sig, tap, w, b, v, vb, mid, z_out):
        for s in tiles(n):
            a = sig[0, :, shift(s, off)]
            filt, gate = gates(w[0], jnp.concatenate([tap[:, s], a], axis=0), b[:, 0:1])
            z = (filt * gate).astype(BF16)
            z_out[:, s] = z
            mid[:, s] = (a.astype(F32) + mm(v[0, :64, :], z) + vb[:64, 0:1]).astype(BF16)

    out = [near(64, n), near(128, n)]
    return call(body, out, 90000 * n, "lower_forward", signal, tap, w, b, v, vb)


def upper_critical(off, n, mid, tap, top, skip, w, b, wt, vt):
    def body(mid, tap, top, skip, w, b, wt, vt, z_out, gpre_out, gdel):
        for s in tiles(n):
            filt, gate = gates(w[1], jnp.concatenate([tap[:, s], mid[:, s]], axis=0), b[:, 1:2])
            z_out[:, s] = (filt * gate).astype(BF16)
            u = jnp.concatenate([top[0, :, shift(s, off)], skip[0, :, shift(s, off)]], axis=0)
            gpre = gate_grad(mm(vt[1], u), filt, gate)
            gpre_out[:, s] = gpre
            gdel[:, s] = mm(wt[1, :64, :], gpre).astype(BF16)

    out = [near(128, n), near(256, n), near(64, n)]
    return call(body, out, 130000 * n, "upper_critical", mid, tap, top, skip, w, b, wt, vt)


def put_sums(out, pieces, before=None):
    conv = sum(mm_t(gpre, stacked) for gpre, _, stacked, _ in pieces)
    proj = sum(mm_t(u, z) for _, u, _, z in pieces)
    bias = sum(jnp.sum(p[0].astype(F32), axis=1, keepdims=True) for p in pieces)
    proj_bias = sum(jnp.sum(p[1].astype(F32), axis=1, keepdims=True) for p in pieces)
    lane = lax.broadcasted_iota(jnp.int32, (128, 128), 1)
    biases = jnp.where(lane == 0, bias[:128], jnp.where(lane == 1, bias[128:], proj_bias))
    for start, value in ((0, conv), (256, proj), (384, jnp.where(lane < 3, biases, 0.0))):
        at = slice(start, start + value.shape[0])
        out[at, :] = value if before is None else before[at, :] + value


def upper_sums(n, mids, taps, gpres, z1s, top, skip):
    h = len(mids)

    def body(*refs):
        mids, taps, gpres, z1s = (refs[i * h : i * h + h] for i in range(4))
        top, skip, sums = refs[4 * h :]
        pieces = []
        for i in range(h):
            at = slice(i * n, i * n + n)
            u = jnp.concatenate([top[0, :, at], skip[0, :, at]], axis=0)
            stacked = jnp.concatenate([taps[i][...], mids[i][...]], axis=0)
            pieces.append((gpres[i][...], u, stacked, z1s[i][...]))
        put_sums(sums, pieces)

    m = h * n
    return call(
        body, [near(512, 128, dtype=F32)], 100000 * m, "upper_sums",
        *mids, *taps, *gpres, *z1s, top, skip,
    )[0]


def upper_outputs(n, mids, z0s, z1s, v, vb):
    h = len(mids)

    def body(*refs):
        mids, z0s, z1s = (refs[i * h : i * h + h] for i in range(3))
        v, vb, x_top, skip_sum = refs[3 * h :]
        both = jnp.concatenate([v[0, 64:, :], v[1, 64:, :]], axis=1)
        both_bias = vb[64:, 0:1] + vb[64:, 1:2]
        for i in range(h):
            for s in tiles(n):
                at = shift(s, i * n)
                z = z1s[i][:, s]
                own = mids[i][:, s].astype(F32) + mm(v[1, :64, :], z) + vb[:64, 1:2]
                x_top[0, :, at] = own.astype(BF16)
                zz = jnp.concatenate([z0s[i][:, s], z], axis=0)
                skip_sum[0, :, at] = (mm(both, zz) + both_bias).astype(BF16)

    m = h * n
    out = [jax.ShapeDtypeStruct((1, 64, m), BF16)] * 2
    return call(body, out, 50000 * m, "upper_outputs", *mids, *z0s, *z1s, v, vb)


def lower_backward(off, n, gdel, gpre1, signal, tap, z0, top, skip, w, b, wt, vt, before):
    def body(gdel, gpre1, sig, tap, z0, top, skip, w, b, wt, vt, *rest):
        pieces = []
        gdel_out, part = rest[len(before) : len(before) + 2]
        if before:
            gdel_out[:, :off] = rest[0][...]
        for s in tiles(n):
            at = shift(s, off)
            own = top[0, :, at].astype(F32) + mm(wt[1, 64:, :], gpre1[:, s])
            grad = (own + gdel[:, s].astype(F32)).astype(BF16)
            both = jnp.concatenate([grad, skip[0, :, at]], axis=0)
            stacked = jnp.concatenate([tap[:, s], sig[0, :, at]], axis=0)
            filt, gate = gates(w[0], stacked, b[:, 0:1])
            gpre = gate_grad(mm(vt[0], both), filt, gate)
            pieces.append((gpre, both, stacked, z0[:, s]))
            gin = mm(wt[0], gpre)
            gdel_out[:, shift(s, gdel_out.shape[1] - n)] = gin[:64].astype(BF16)
            part[:, s] = grad.astype(F32) + gin[64:]
        if before:
            _, sums, high, _, _, give, keep = rest
            put_sums(keep, pieces, sums)
            low, high = keep[...], high[...]
            own = jnp.broadcast_to(lax.axis_index("core") == 0, low.shape)
            give[...] = jnp.where(own, high, low)
            keep[...] = jnp.where(own, low, high)
        else:
            put_sums(rest[-1], pieces)

    out = [near(64, off + n), near(64, n, dtype=F32)]
    out += [near(512, 128, dtype=F32)] * (2 if before else 1)
    return call(
        body, out, 320000 * n, "lower_backward",
        gdel, gpre1, signal, tap, z0, top, skip, w, b, wt, vt, *before,
    )


def place(held, other):
    def body(held, other, conv, conv_bias, proj, proj_bias):
        a, b = held[...], other[...]
        own = jnp.broadcast_to(lax.axis_index("core") == 0, a.shape)
        for layer, rows in enumerate((jnp.where(own, a, b), jnp.where(own, b, a))):
            conv[layer] = rows[:256]
            proj[layer] = rows[256:384]
            biases = jnp.transpose(rows[384:])
            conv_bias[layer : layer + 1, :128] = biases[0:1]
            conv_bias[layer : layer + 1, 128:] = biases[1:2]
            proj_bias[layer : layer + 1, :] = biases[2:3]

    out = [jax.ShapeDtypeStruct(d, F32) for d in ((2, 256, 128), (2, 256), (2, 128, 128), (2, 128))]
    return call(body, out, 1000, "place", held, other)


def swap_cores(block):
    return lax.ppermute(block, "core", [(0, 1), (1, 0)])


def add(x, y):
    def body(x, y, out):
        out[...] = x[...] + y[...]

    return call(body, [near(*x.shape, dtype=F32)], 1000, "add", x, y)[0]


def finish(parts, later):
    n = parts[0].shape[1]

    def body(*refs):
        far, out = refs[-2:]
        for i, own in enumerate(refs[:-2]):
            at = slice(i * n, i * n + n)
            out[0, :, at] = (own[...] + far[:, at].astype(F32)).astype(BF16)

    return call(body, [near(1, *later.shape)], 1000, "finish", *parts, later)[0]


def share_out(parts, copies, scale=1.0):
    def body(parts, out):
        total = parts[0]
        for i in range(1, parts.shape[0]):
            total += parts[i]
        total *= scale
        for i in range(copies):
            out[i] = total

    out = [near(copies, *parts.shape[1:], dtype=F32)]
    return call(body, out, 1000, "share_out", parts)[0]


def on_device(signal, w, b, v, vb, top, skip):
    m = signal.shape[2]
    n = m // HALVES
    offs = range(0, m, n)
    taps = [from_behind(signal[0, :, o : o + n], 1) for o in offs]
    b, vb, wt, vt = prepare(w, b, v, vb)
    mids, z0s, mid_taps = [], [], []
    for o, tap in zip(offs, taps):
        mid, z0 = lower_forward(o, n, signal, tap, w, b, v, vb)
        mids.append(mid)
        z0s.append(z0)
        mid_taps.append(from_behind(mid, 2))
    z1s, gpres1, gdels1 = [], [], []
    for o, mid, tap in zip(offs, mids, mid_taps):
        z1, gpre1, gdel = upper_critical(o, n, mid, tap, top, skip, w, b, wt, vt)
        z1s.append(z1)
        gpres1.append(gpre1)
        gdels1.append(from_behind(gdel, -2))
    args = lambda i: [(o, n, d, g, signal, t, z, top, skip, w, b, wt, vt)
            for o, d, g, t, z in zip(offs, gdels1, gpres1, taps, z0s)][i]
    gdel_a, part_a, sums = lower_backward(*args(0), [])
    z1s, sums = lax.optimization_barrier((z1s, sums))
    high = upper_sums(n, mids, mid_taps, gpres1, z1s, top, skip)
    z1s, high = lax.optimization_barrier((z1s, high))
    x_top, skip_sum = upper_outputs(n, mids, z0s, z1s, v, vb)
    gdels1[1], x_top, skip_sum = lax.optimization_barrier((gdels1[1], x_top, skip_sum))
    gdel0, part_b, give, keep = lower_backward(*args(1), [gdel_a, sums, high])
    count = signal.shape[0] * lax.axis_size(CORNER) * m * lax.axis_size(TM)
    plane, depth = lax.axis_size(PLANE), lax.axis_size("z")
    scale = 1.0 / math.sqrt(count)
    rows = add(keep, swap_cores(give)).reshape(plane, -1, 128)
    rows, gdel0 = lax.optimization_barrier((rows, gdel0))
    later = from_behind(gdel0, -1)
    parts = lax.all_to_all(rows, PLANE, 0, 0, tiled=True)
    parts = share_out(parts, depth)
    parts = lax.all_to_all(parts, "z", 0, 0, tiled=True)
    parts = share_out(parts, plane, scale)
    held = lax.all_to_all(parts, PLANE, 0, 0, tiled=True).reshape(give.shape)
    grad_input = finish([part_a, part_b], later)
    return (x_top, skip_sum, grad_input, *place(held, swap_cores(held)))


def solution(mesh):
    fine = Mesh(mesh.devices.reshape(4, 2, 2, 8, 2), ("y", "xl", "core", "z", "xh"))
    field = P(CORNER, None, TM)
    return jax.shard_map(
        on_device,
        mesh=fine,
        in_specs=(field, P(), P(), P(), P(), field, field),
        out_specs=(field, field, field, P(), P(), P(), P()),
        check_vma=False,
    )
```

```python
import math

import jax
import jax.numpy as jnp
from jax import lax
from jax.experimental import pallas as pl
from jax.experimental.pallas import tpu as pltpu
from jax.sharding import Mesh, PartitionSpec as P

CORNER = ("y", "xl", "core")
TM = ("z", "xh")
PLANE = ("y", "xl", "xh")
HALVES = 2
TILE = 2048
F32, BF16 = jnp.float32, jnp.bfloat16


def from_behind(block, distance):
    devices = range(lax.axis_size(TM))
    route = [(i - distance, i) for i in devices if i - distance in devices]
    return lax.ppermute(block, TM, route)


def mm(a, b):
    return lax.dot_general(a, b, (((1,), (0,)), ((), ())), preferred_element_type=F32)


def mm_t(a, b):
    return lax.dot_general(a, b, (((1,), (1,)), ((), ())), preferred_element_type=F32)


def gates(weight, stacked, bias):
    pre = mm(weight, stacked) + bias
    half = pre.shape[0] // 2
    return jnp.tanh(pre[:half]), 0.5 * jnp.tanh(0.5 * pre[half:]) + 0.5


def gate_grad(gz, filt, gate):
    both = gz * gate
    return jnp.concatenate(
        [both * (1.0 - filt * filt), both * filt * (1.0 - gate)], axis=0
    ).astype(BF16)


def tiles(n):
    return [slice(i, i + TILE) for i in range(0, n, TILE)]


def shift(s, off):
    return slice(s.start + off, s.stop + off)


def call(body, out, flops, name, *args):
    size = sum(math.prod(a.shape) * a.dtype.itemsize for a in (*args, *out))
    spec = pl.BlockSpec(memory_space=pltpu.VMEM)
    return pl.pallas_call(
        body,
        out_shape=out,
        in_specs=[spec] * len(args),
        out_specs=[spec] * len(out),
        name=name,
        cost_estimate=pl.CostEstimate(flops=flops, bytes_accessed=size, transcendentals=0),
        compiler_params=pltpu.CompilerParams(vmem_limit_bytes=12 * 2**20),
    )(*args)


def near(*shape, dtype=BF16):
    return jax.ShapeDtypeStruct(shape, dtype)


def prepare(w, b, v, vb):
    def body(w, b, v, vb, b_out, vb_out, wt, vt):
        for rows, out in ((b, b_out), (vb, vb_out)):
            out[...] = jnp.transpose(jnp.tile(rows[...], (4, 1)))
        for layer in range(2):
            wt[layer] = jnp.transpose(w[layer])
            vt[layer] = jnp.transpose(v[layer])

    out = [near(256, 8, dtype=F32), near(128, 8, dtype=F32), near(2, 128, 256), near(2, 128, 128)]
    return call(body, out, 1000, "prepare", w, b, v, vb)


def lower_forward(off, n, signal, tap, w, b, v, vb):
    def body(sig, tap, w, b, v, vb, mid, z_out):
        for s in tiles(n):
            a = sig[0, :, shift(s, off)]
            filt, gate = gates(w[0], jnp.concatenate([tap[:, s], a], axis=0), b[:, 0:1])
            z = (filt * gate).astype(BF16)
            z_out[:, s] = z
            mid[:, s] = (a.astype(F32) + mm(v[0, :64, :], z) + vb[:64, 0:1]).astype(BF16)

    out = [near(64, n), near(128, n)]
    return call(body, out, 90000 * n, "lower_forward", signal, tap, w, b, v, vb)


def upper_critical(off, n, mid, tap, top, skip, w, b, wt, vt):
    def body(mid, tap, top, skip, w, b, wt, vt, z_out, gpre_out, gdel):
        for s in tiles(n):
            filt, gate = gates(w[1], jnp.concatenate([tap[:, s], mid[:, s]], axis=0), b[:, 1:2])
            z_out[:, s] = (filt * gate).astype(BF16)
            u = jnp.concatenate([top[0, :, shift(s, off)], skip[0, :, shift(s, off)]], axis=0)
            gpre = gate_grad(mm(vt[1], u), filt, gate)
            gpre_out[:, s] = gpre
            gdel[:, s] = mm(wt[1, :64, :], gpre).astype(BF16)

    out = [near(128, n), near(256, n), near(64, n)]
    return call(body, out, 130000 * n, "upper_critical", mid, tap, top, skip, w, b, wt, vt)


def put_sums(out, pieces, before=None):
    conv = sum(mm_t(gpre, stacked) for gpre, _, stacked, _ in pieces)
    proj = sum(mm_t(u, z) for _, u, _, z in pieces)
    bias = sum(jnp.sum(p[0].astype(F32), axis=1, keepdims=True) for p in pieces)
    proj_bias = sum(jnp.sum(p[1].astype(F32), axis=1, keepdims=True) for p in pieces)
    lane = lax.broadcasted_iota(jnp.int32, (128, 128), 1)
    biases = jnp.where(lane == 0, bias[:128], jnp.where(lane == 1, bias[128:], proj_bias))
    for start, value in ((0, conv), (256, proj), (384, jnp.where(lane < 3, biases, 0.0))):
        at = slice(start, start + value.shape[0])
        out[at, :] = value if before is None else before[at, :] + value


def upper_sums(n, mids, taps, gpres, z1s, top, skip):
    h = len(mids)

    def body(*refs):
        mids, taps, gpres, z1s = (refs[i * h : i * h + h] for i in range(4))
        top, skip, sums = refs[4 * h :]
        pieces = []
        for i in range(h):
            at = slice(i * n, i * n + n)
            u = jnp.concatenate([top[0, :, at], skip[0, :, at]], axis=0)
            stacked = jnp.concatenate([taps[i][...], mids[i][...]], axis=0)
            pieces.append((gpres[i][...], u, stacked, z1s[i][...]))
        put_sums(sums, pieces)

    m = h * n
    return call(
        body, [near(512, 128, dtype=F32)], 100000 * m, "upper_sums",
        *mids, *taps, *gpres, *z1s, top, skip,
    )[0]


def upper_outputs(n, mids, z0s, z1s, v, vb):
    h = len(mids)

    def body(*refs):
        mids, z0s, z1s = (refs[i * h : i * h + h] for i in range(3))
        v, vb, x_top, skip_sum = refs[3 * h :]
        both = jnp.concatenate([v[0, 64:, :], v[1, 64:, :]], axis=1)
        both_bias = vb[64:, 0:1] + vb[64:, 1:2]
        for i in range(h):
            for s in tiles(n):
                at = shift(s, i * n)
                z = z1s[i][:, s]
                own = mids[i][:, s].astype(F32) + mm(v[1, :64, :], z) + vb[:64, 1:2]
                x_top[0, :, at] = own.astype(BF16)
                zz = jnp.concatenate([z0s[i][:, s], z], axis=0)
                skip_sum[0, :, at] = (mm(both, zz) + both_bias).astype(BF16)

    m = h * n
    out = [jax.ShapeDtypeStruct((1, 64, m), BF16)] * 2
    return call(body, out, 50000 * m, "upper_outputs", *mids, *z0s, *z1s, v, vb)


def lower_backward(off, n, gdel, gpre1, signal, tap, z0, top, skip, w, b, wt, vt, before):
    def body(gdel, gpre1, sig, tap, z0, top, skip, w, b, wt, vt, *rest):
        pieces = []
        gdel_out, part = rest[len(before) : len(before) + 2]
        if before:
            gdel_out[:, :off] = rest[0][...]
        for s in tiles(n):
            at = shift(s, off)
            own = top[0, :, at].astype(F32) + mm(wt[1, 64:, :], gpre1[:, s])
            grad = (own + gdel[:, s].astype(F32)).astype(BF16)
            both = jnp.concatenate([grad, skip[0, :, at]], axis=0)
            stacked = jnp.concatenate([tap[:, s], sig[0, :, at]], axis=0)
            filt, gate = gates(w[0], stacked, b[:, 0:1])
            gpre = gate_grad(mm(vt[0], both), filt, gate)
            pieces.append((gpre, both, stacked, z0[:, s]))
            gin = mm(wt[0], gpre)
            gdel_out[:, shift(s, gdel_out.shape[1] - n)] = gin[:64].astype(BF16)
            part[:, s] = grad.astype(F32) + gin[64:]
        if before:
            _, sums, high, _, _, give, keep = rest
            put_sums(keep, pieces, sums)
            low, high = keep[...], high[...]
            own = jnp.broadcast_to(lax.axis_index("core") == 0, low.shape)
            give[...] = jnp.where(own, high, low)
            keep[...] = jnp.where(own, low, high)
        else:
            put_sums(rest[-1], pieces)

    out = [near(64, off + n), near(64, n, dtype=F32)]
    out += [near(512, 128, dtype=F32)] * (2 if before else 1)
    return call(
        body, out, 320000 * n, "lower_backward",
        gdel, gpre1, signal, tap, z0, top, skip, w, b, wt, vt, *before,
    )


def place(held, other):
    def body(held, other, conv, conv_bias, proj, proj_bias):
        a, b = held[...], other[...]
        own = jnp.broadcast_to(lax.axis_index("core") == 0, a.shape)
        for layer, rows in enumerate((jnp.where(own, a, b), jnp.where(own, b, a))):
            conv[layer] = rows[:256]
            proj[layer] = rows[256:384]
            biases = jnp.transpose(rows[384:])
            conv_bias[layer : layer + 1, :128] = biases[0:1]
            conv_bias[layer : layer + 1, 128:] = biases[1:2]
            proj_bias[layer : layer + 1, :] = biases[2:3]

    out = [jax.ShapeDtypeStruct(d, F32) for d in ((2, 256, 128), (2, 256), (2, 128, 128), (2, 128))]
    return call(body, out, 1000, "place", held, other)


def swap_cores(block):
    return lax.ppermute(block, "core", [(0, 1), (1, 0)])


def add(x, y):
    def body(x, y, out):
        out[...] = x[...] + y[...]

    return call(body, [near(*x.shape, dtype=F32)], 1000, "add", x, y)[0]


def finish(parts, later):
    n = parts[0].shape[1]

    def body(*refs):
        far, out = refs[-2:]
        for i, own in enumerate(refs[:-2]):
            at = slice(i * n, i * n + n)
            out[0, :, at] = (own[...] + far[:, at].astype(F32)).astype(BF16)

    return call(body, [near(1, *later.shape)], 1000, "finish", *parts, later)[0]


def share_out(parts, copies, scale=1.0):
    def body(parts, out):
        total = parts[0]
        for i in range(1, parts.shape[0]):
            total += parts[i]
        total *= scale
        for i in range(copies):
            out[i] = total

    out = [near(copies, *parts.shape[1:], dtype=F32)]
    return call(body, out, 1000, "share_out", parts)[0]


def on_device(signal, w, b, v, vb, top, skip):
    m = signal.shape[2]
    n = m // HALVES
    offs = range(0, m, n)
    again = lax.optimization_barrier(signal)
    taps = [from_behind((again if o else signal)[0, :, o : o + n], 1) for o in offs]
    b, vb, wt, vt = prepare(w, b, v, vb)
    mids, z0s, mid_taps = [], [], []
    for o, tap in zip(offs, taps):
        mid, z0 = lower_forward(o, n, signal, tap, w, b, v, vb)
        mids.append(mid)
        z0s.append(z0)
        mid_taps.append(from_behind(mid, 2))
    z1s, gpres1, gdels1 = [], [], []
    for o, mid, tap in zip(offs, mids, mid_taps):
        z1, gpre1, gdel = upper_critical(o, n, mid, tap, top, skip, w, b, wt, vt)
        z1s.append(z1)
        gpres1.append(gpre1)
        gdels1.append(from_behind(gdel, -2))
    args = lambda i: [(o, n, d, g, signal, t, z, top, skip, w, b, wt, vt)
            for o, d, g, t, z in zip(offs, gdels1, gpres1, taps, z0s)][i]
    gdel_a, part_a, sums = lower_backward(*args(0), [])
    z1s, sums = lax.optimization_barrier((z1s, sums))
    high = upper_sums(n, mids, mid_taps, gpres1, z1s, top, skip)
    z1s, high = lax.optimization_barrier((z1s, high))
    x_top, skip_sum = upper_outputs(n, mids, z0s, z1s, v, vb)
    gdels1[1], x_top, skip_sum = lax.optimization_barrier((gdels1[1], x_top, skip_sum))
    gdel0, part_b, give, keep = lower_backward(*args(1), [gdel_a, sums, high])
    count = signal.shape[0] * lax.axis_size(CORNER) * m * lax.axis_size(TM)
    plane, depth = lax.axis_size(PLANE), lax.axis_size("z")
    scale = 1.0 / math.sqrt(count)
    rows = add(keep, swap_cores(give)).reshape(plane, -1, 128)
    rows, gdel0 = lax.optimization_barrier((rows, gdel0))
    later = from_behind(gdel0, -1)
    parts = lax.all_to_all(rows, PLANE, 0, 0, tiled=True)
    parts = share_out(parts, depth)
    parts = lax.all_to_all(parts, "z", 0, 0, tiled=True)
    parts = share_out(parts, plane, scale)
    held = lax.all_to_all(parts, PLANE, 0, 0, tiled=True).reshape(give.shape)
    grad_input = finish([part_a, part_b], later)
    return (x_top, skip_sum, grad_input, *place(held, swap_cores(held)))


def solution(mesh):
    fine = Mesh(mesh.devices.reshape(4, 2, 2, 8, 2), ("y", "xl", "core", "z", "xh"))
    field = P(CORNER, None, TM)
    return jax.shard_map(
        on_device,
        mesh=fine,
        in_specs=(field, P(), P(), P(), P(), field, field),
        out_specs=(field, field, field, P(), P(), P(), P()),
        check_vma=False,
    )
```

```python
import math

import jax
import jax.numpy as jnp
from jax import lax
from jax.experimental import pallas as pl
from jax.experimental.pallas import tpu as pltpu
from jax.sharding import Mesh, PartitionSpec as P

CORNER = ("y", "xl", "core")
TM = ("z", "xh")
PLANE = ("y", "xl", "xh")
HALVES = 2
TILE = 2048
F32, BF16 = jnp.float32, jnp.bfloat16


def from_behind(block, distance):
    devices = range(lax.axis_size(TM))
    route = [(i - distance, i) for i in devices if i - distance in devices]
    return lax.ppermute(block, TM, route)


def mm(a, b):
    return lax.dot_general(a, b, (((1,), (0,)), ((), ())), preferred_element_type=F32)


def mm_t(a, b):
    return lax.dot_general(a, b, (((1,), (1,)), ((), ())), preferred_element_type=F32)


def gates(weight, stacked, bias):
    pre = mm(weight, stacked) + bias
    half = pre.shape[0] // 2
    return jnp.tanh(pre[:half]), 0.5 * jnp.tanh(0.5 * pre[half:]) + 0.5


def gate_grad(gz, filt, gate):
    both = gz * gate
    return jnp.concatenate(
        [both * (1.0 - filt * filt), both * filt * (1.0 - gate)], axis=0
    ).astype(BF16)


def tiles(n):
    return [slice(i, i + TILE) for i in range(0, n, TILE)]


def shift(s, off):
    return slice(s.start + off, s.stop + off)


def call(body, out, flops, name, *args):
    size = sum(math.prod(a.shape) * a.dtype.itemsize for a in (*args, *out))
    spec = pl.BlockSpec(memory_space=pltpu.VMEM)
    return pl.pallas_call(
        body,
        out_shape=out,
        in_specs=[spec] * len(args),
        out_specs=[spec] * len(out),
        name=name,
        cost_estimate=pl.CostEstimate(flops=flops, bytes_accessed=size, transcendentals=0),
        compiler_params=pltpu.CompilerParams(vmem_limit_bytes=12 * 2**20),
    )(*args)


def near(*shape, dtype=BF16):
    return jax.ShapeDtypeStruct(shape, dtype)


def prepare(w, b, v, vb):
    def body(w, b, v, vb, b_out, vb_out, wt, vt):
        for rows, out in ((b, b_out), (vb, vb_out)):
            out[...] = jnp.transpose(jnp.tile(rows[...], (4, 1)))
        for layer in range(2):
            wt[layer] = jnp.transpose(w[layer])
            vt[layer] = jnp.transpose(v[layer])

    out = [near(256, 8, dtype=F32), near(128, 8, dtype=F32), near(2, 128, 256), near(2, 128, 128)]
    return call(body, out, 1000, "prepare", w, b, v, vb)


def lower_forward(off, n, signal, tap, w, b, v, vb):
    def body(sig, tap, w, b, v, vb, mid, z_out):
        for s in tiles(n):
            a = sig[0, :, shift(s, off)]
            filt, gate = gates(w[0], jnp.concatenate([tap[:, s], a], axis=0), b[:, 0:1])
            z = (filt * gate).astype(BF16)
            z_out[:, s] = z
            mid[:, s] = (a.astype(F32) + mm(v[0, :64, :], z) + vb[:64, 0:1]).astype(BF16)

    out = [near(64, n), near(128, n)]
    return call(body, out, 90000 * n, "lower_forward", signal, tap, w, b, v, vb)


def upper_critical(off, n, mid, tap, top, skip, w, b, wt, vt):
    def body(mid, tap, top, skip, w, b, wt, vt, z_out, gpre_out, gdel):
        for s in tiles(n):
            filt, gate = gates(w[1], jnp.concatenate([tap[:, s], mid[:, s]], axis=0), b[:, 1:2])
            z_out[:, s] = (filt * gate).astype(BF16)
            u = jnp.concatenate([top[0, :, shift(s, off)], skip[0, :, shift(s, off)]], axis=0)
            gpre = gate_grad(mm(vt[1], u), filt, gate)
            gpre_out[:, s] = gpre
            gdel[:, s] = mm(wt[1, :64, :], gpre).astype(BF16)

    out = [near(128, n), near(256, n), near(64, n)]
    return call(body, out, 130000 * n, "upper_critical", mid, tap, top, skip, w, b, wt, vt)


def put_sums(out, pieces, before=None):
    conv = sum(mm_t(gpre, stacked) for gpre, _, stacked, _ in pieces)
    proj = sum(mm_t(u, z) for _, u, _, z in pieces)
    bias = sum(jnp.sum(p[0].astype(F32), axis=1, keepdims=True) for p in pieces)
    proj_bias = sum(jnp.sum(p[1].astype(F32), axis=1, keepdims=True) for p in pieces)
    lane = lax.broadcasted_iota(jnp.int32, (128, 128), 1)
    biases = jnp.where(lane == 0, bias[:128], jnp.where(lane == 1, bias[128:], proj_bias))
    for start, value in ((0, conv), (256, proj), (384, jnp.where(lane < 3, biases, 0.0))):
        at = slice(start, start + value.shape[0])
        out[at, :] = value if before is None else before[at, :] + value


def upper_sums(n, mids, taps, gpres, z1s, top, skip):
    h = len(mids)

    def body(*refs):
        mids, taps, gpres, z1s = (refs[i * h : i * h + h] for i in range(4))
        top, skip, sums = refs[4 * h :]
        pieces = []
        for i in range(h):
            at = slice(i * n, i * n + n)
            u = jnp.concatenate([top[0, :, at], skip[0, :, at]], axis=0)
            stacked = jnp.concatenate([taps[i][...], mids[i][...]], axis=0)
            pieces.append((gpres[i][...], u, stacked, z1s[i][...]))
        put_sums(sums, pieces)

    m = h * n
    return call(
        body, [near(512, 128, dtype=F32)], 100000 * m, "upper_sums",
        *mids, *taps, *gpres, *z1s, top, skip,
    )[0]


def upper_outputs(n, mids, z0s, z1s, v, vb):
    h = len(mids)

    def body(*refs):
        mids, z0s, z1s = (refs[i * h : i * h + h] for i in range(3))
        v, vb, x_top, skip_sum = refs[3 * h :]
        both = jnp.concatenate([v[0, 64:, :], v[1, 64:, :]], axis=1)
        both_bias = vb[64:, 0:1] + vb[64:, 1:2]
        for i in range(h):
            for s in tiles(n):
                at = shift(s, i * n)
                z = z1s[i][:, s]
                own = mids[i][:, s].astype(F32) + mm(v[1, :64, :], z) + vb[:64, 1:2]
                x_top[0, :, at] = own.astype(BF16)
                zz = jnp.concatenate([z0s[i][:, s], z], axis=0)
                skip_sum[0, :, at] = (mm(both, zz) + both_bias).astype(BF16)

    m = h * n
    out = [jax.ShapeDtypeStruct((1, 64, m), BF16)] * 2
    return call(body, out, 50000 * m, "upper_outputs", *mids, *z0s, *z1s, v, vb)


def lower_backward(off, n, gdel, gpre1, signal, tap, z0, top, skip, w, b, wt, vt, before):
    def body(gdel, gpre1, sig, tap, z0, top, skip, w, b, wt, vt, *rest):
        pieces = []
        gdel_out, part = rest[len(before) : len(before) + 2]
        if before:
            gdel_out[:, :off] = rest[0][...]
        for s in tiles(n):
            at = shift(s, off)
            own = top[0, :, at].astype(F32) + mm(wt[1, 64:, :], gpre1[:, s])
            grad = (own + gdel[:, s].astype(F32)).astype(BF16)
            both = jnp.concatenate([grad, skip[0, :, at]], axis=0)
            stacked = jnp.concatenate([tap[:, s], sig[0, :, at]], axis=0)
            filt, gate = gates(w[0], stacked, b[:, 0:1])
            gpre = gate_grad(mm(vt[0], both), filt, gate)
            pieces.append((gpre, both, stacked, z0[:, s]))
            gin = mm(wt[0], gpre)
            gdel_out[:, shift(s, gdel_out.shape[1] - n)] = gin[:64].astype(BF16)
            part[:, s] = grad.astype(F32) + gin[64:]
        if before:
            _, sums, high, _, _, give, keep = rest
            put_sums(keep, pieces, sums)
            low, high = keep[...], high[...]
            own = jnp.broadcast_to(lax.axis_index("core") == 0, low.shape)
            give[...] = jnp.where(own, high, low)
            keep[...] = jnp.where(own, low, high)
        else:
            put_sums(rest[-1], pieces)

    out = [near(64, off + n), near(64, n, dtype=F32)]
    out += [near(512, 128, dtype=F32)] * (2 if before else 1)
    return call(
        body, out, 320000 * n, "lower_backward",
        gdel, gpre1, signal, tap, z0, top, skip, w, b, wt, vt, *before,
    )


def place(held, other):
    def body(held, other, conv, conv_bias, proj, proj_bias):
        a, b = held[...].astype(F32), other[...].astype(F32)
        own = jnp.broadcast_to(lax.axis_index("core") == 0, a.shape)
        for layer, rows in enumerate((jnp.where(own, a, b), jnp.where(own, b, a))):
            conv[layer] = rows[:256]
            proj[layer] = rows[256:384]
            biases = jnp.transpose(rows[384:])
            conv_bias[layer : layer + 1, :128] = biases[0:1]
            conv_bias[layer : layer + 1, 128:] = biases[1:2]
            proj_bias[layer : layer + 1, :] = biases[2:3]

    out = [jax.ShapeDtypeStruct(d, F32) for d in ((2, 256, 128), (2, 256), (2, 128, 128), (2, 128))]
    return call(body, out, 1000, "place", held, other)


def swap_cores(block):
    return lax.ppermute(block, "core", [(0, 1), (1, 0)])


def add(x, y):
    def body(x, y, out):
        out[...] = x[...] + y[...]

    return call(body, [near(*x.shape, dtype=F32)], 1000, "add", x, y)[0]


def finish(parts, later):
    n = parts[0].shape[1]

    def body(*refs):
        far, out = refs[-2:]
        for i, own in enumerate(refs[:-2]):
            at = slice(i * n, i * n + n)
            out[0, :, at] = (own[...] + far[:, at].astype(F32)).astype(BF16)

    return call(body, [near(1, *later.shape)], 1000, "finish", *parts, later)[0]


def share_out(parts, copies, scale=1.0, dtype=F32):
    def body(parts, out):
        total = parts[0]
        for i in range(1, parts.shape[0]):
            total += parts[i]
        total *= scale
        for i in range(copies):
            out[i] = total.astype(dtype)

    out = [near(copies, *parts.shape[1:], dtype=dtype)]
    return call(body, out, 1000, "share_out", parts)[0]


def on_device(signal, w, b, v, vb, top, skip):
    m = signal.shape[2]
    n = m // HALVES
    offs = range(0, m, n)
    taps = [from_behind(signal[0, :, o : o + n], 1) for o in offs]
    b, vb, wt, vt = prepare(w, b, v, vb)
    mids, z0s, mid_taps = [], [], []
    for o, tap in zip(offs, taps):
        mid, z0 = lower_forward(o, n, signal, tap, w, b, v, vb)
        mids.append(mid)
        z0s.append(z0)
        mid_taps.append(from_behind(mid, 2))
    z1s, gpres1, gdels1 = [], [], []
    for o, mid, tap in zip(offs, mids, mid_taps):
        z1, gpre1, gdel = upper_critical(o, n, mid, tap, top, skip, w, b, wt, vt)
        z1s.append(z1)
        gpres1.append(gpre1)
        gdels1.append(from_behind(gdel, -2))
    args = lambda i: [(o, n, d, g, signal, t, z, top, skip, w, b, wt, vt)
            for o, d, g, t, z in zip(offs, gdels1, gpres1, taps, z0s)][i]
    gdel_a, part_a, sums = lower_backward(*args(0), [])
    z1s, sums = lax.optimization_barrier((z1s, sums))
    high = upper_sums(n, mids, mid_taps, gpres1, z1s, top, skip)
    z1s, high = lax.optimization_barrier((z1s, high))
    x_top, skip_sum = upper_outputs(n, mids, z0s, z1s, v, vb)
    gdels1[1], x_top, skip_sum = lax.optimization_barrier((gdels1[1], x_top, skip_sum))
    gdel0, part_b, give, keep = lower_backward(*args(1), [gdel_a, sums, high])
    count = signal.shape[0] * lax.axis_size(CORNER) * m * lax.axis_size(TM)
    plane, depth = lax.axis_size(PLANE), lax.axis_size("z")
    scale = 1.0 / math.sqrt(count)
    rows = add(keep, swap_cores(give)).reshape(plane, -1, 128)
    rows, gdel0 = lax.optimization_barrier((rows, gdel0))
    later = from_behind(gdel0, -1)
    parts = lax.all_to_all(rows, PLANE, 0, 0, tiled=True)
    parts = share_out(parts, depth)
    parts = lax.all_to_all(parts, "z", 0, 0, tiled=True)
    parts = share_out(parts, plane, scale, BF16)
    held = lax.all_to_all(parts, PLANE, 0, 0, tiled=True).reshape(give.shape)
    grad_input = finish([part_a, part_b], later)
    return (x_top, skip_sum, grad_input, *place(held, swap_cores(held)))


def solution(mesh):
    fine = Mesh(mesh.devices.reshape(4, 2, 2, 8, 2), ("y", "xl", "core", "z", "xh"))
    field = P(CORNER, None, TM)
    return jax.shard_map(
        on_device,
        mesh=fine,
        in_specs=(field, P(), P(), P(), P(), field, field),
        out_specs=(field, field, field, P(), P(), P(), P()),
        check_vma=False,
    )
```
